32 devices in a mesh: dp: 16 (over z, y, x), tensor: 2 (over core).
Axes of the slice: x: 2, y: 2, z: 4, core: 2. Of those that a mesh axis runs over, the one named last changes fastest.
Arguments:
- layer_input: bfloat16 [640, 5120], P('dp', 'tensor'), may hold values from -6 to 6
- up_weight: bfloat16 [5120, 13824], P('dp', 'tensor'), may hold values from -0.078125 to 0.078125
- grad_output: bfloat16 [640, 13824], P('dp', 'tensor'), may hold values from -60 to 60
- factor_input: float32 [5120, 5120], P('dp', 'tensor'), may hold values from -4 to 15, as said below
- factor_grad: float32 [13824, 13824], P('dp', 'tensor'), may hold values from -4 to 15, as said below
- decay: float32 [1], replicated, may hold values from 0.5 to 0.95
Outputs:
- grad_weight: float32 [5120, 13824], P('dp', 'tensor')
- grad_input: bfloat16 [640, 5120], P('tensor', 'dp')
- new_factor_input: float32 [5120, 5120], P('dp', 'tensor')
- new_factor_grad: float32 [13824, 13824], P('dp', 'tensor')
The draws below stay inside these ranges and needn't reach their ends.
Inputs may be any that keep to these rules, and one draw needn't show every extreme that they name: `factor_input`: symmetric. `factor_grad`: symmetric.
All inputs are finite; a program needn't handle non-finite values.
Results may differ from the reference program's by a relative error of at most 0.001.
Values may be sent and summed in bfloat16 or wider, within the bound.
A program may use at most 128 MiB of HBM per device.

```python
import math
import jax
import jax.numpy as jnp
from jax import lax

D = 5120
FF = 13824
TOKENS = 640


def draw_grad_output(key, part):
    first = jax.random.fold_in(key, 11)
    second = jax.random.fold_in(key, 12)
    third = jax.random.fold_in(key, 13)
    row_scale = jnp.exp(jax.random.uniform(second, (TOKENS, 1), jnp.float32, math.log(0.3), math.log(3.0)))
    col_scale = jnp.exp(jax.random.uniform(third, (1, FF), jnp.float32, math.log(0.3), math.log(3.0)))
    base = jnp.clip(jax.random.normal(first, (TOKENS, FF), jnp.float32), -6.0, 6.0)
    return (base * row_scale * col_scale).astype(jnp.bfloat16)


def symmetric_factor(key, order):
    first = jax.random.fold_in(key, 21)
    second = jax.random.fold_in(key, 22)
    loose = jnp.clip(jax.random.normal(first, (order, order), jnp.float32), -4.0, 4.0) * 0.3
    middle = 0.5 * (loose + loose.T)
    lead = jnp.exp(jax.random.uniform(second, (order,), jnp.float32, 0.0, math.log(10.0)))
    return middle + jnp.diag(lead)


def draw_factor_input(key, part):
    return symmetric_factor(jax.random.fold_in(key, 31), D)


def draw_factor_grad(key, part):
    return symmetric_factor(jax.random.fold_in(key, 32), FF)


def level_of(own_key, dims, cuts, smallest, top_value):
    factor_of, own = 1.0, jax.random.fold_in(own_key, 6)
    for position, shards_of in cuts:
        draws = jnp.exp(jax.random.uniform(jax.random.fold_in(own, position), (shards_of,), jnp.float32, smallest / len(cuts), top_value / len(cuts)))
        factor_of = factor_of * jnp.repeat(draws, dims[position] // shards_of).reshape([-1 if axis == position else 1 for axis in range(len(dims))])
    return factor_of


def noise(stream_key, extent, width, limit, cuts=(), kind=jnp.bfloat16):
    gain = level_of(stream_key, extent, cuts, -0.22, 0.18) if cuts else 1.0
    result = jax.random.normal(stream_key, extent, jnp.float32) * width * gain
    return jnp.minimum(jnp.maximum(result, -limit), limit).astype(kind)


def setup_inputs(seed: int = 0) -> dict:
    splits = jax.random.split(jax.random.key(seed), 7)
    layer_input = noise(splits[0], (TOKENS, D), 1.0, 6.0, ((0, 16), (1, 2)))
    up_weight = noise(splits[1], (D, FF), D ** -0.5, 0.078125, ((0, 16), (1, 2)))
    grad_output = draw_grad_output(jax.random.fold_in(splits[6], 71), 0)
    factor_input = draw_factor_input(jax.random.fold_in(splits[6], 71), 0)
    factor_grad = draw_factor_grad(jax.random.fold_in(splits[6], 71), 0)
    decay = jnp.clip(jax.random.uniform(splits[5], (1,), jnp.float32, 0.5, 0.95), 0.5, 0.95)
    return dict(layer_input=layer_input, up_weight=up_weight, grad_output=grad_output, factor_input=factor_input, factor_grad=factor_grad, decay=decay)


def contract_rows(left, right):
    return lax.dot_general(left.astype(jnp.float32), right.astype(jnp.float32), (((0,), (0,)), ((), ())), preferred_element_type=jnp.float32)


def reference(layer_input, up_weight, grad_output, factor_input, factor_grad, decay):
    keep = decay[0]
    blend = (1.0 - keep) / TOKENS
    grad_weight = contract_rows(layer_input, grad_output)
    grad_input = lax.dot_general(grad_output.astype(jnp.float32), up_weight.astype(jnp.float32), (((1,), (1,)), ((), ())), preferred_element_type=jnp.float32).astype(jnp.bfloat16)
    new_factor_input = keep * factor_input + blend * contract_rows(layer_input, layer_input)
    new_factor_grad = keep * factor_grad + blend * contract_rows(grad_output, grad_output)
    return grad_weight, grad_input, new_factor_input, new_factor_grad
```

```python
import functools

import jax
import jax.numpy as jnp
from jax import lax
from jax.experimental import pallas as pl
from jax.experimental.pallas import tpu as pltpu
from jax.sharding import PartitionSpec as P

LANES = 128


def contract_rows(left, right):
    return lax.dot_general(
        left, right, (((0,), (0,)), ((), ())), preferred_element_type=jnp.float32
    )


def contract_cols(left, right):
    return lax.dot_general(
        left, right, (((1,), (1,)), ((), ())), preferred_element_type=jnp.float32
    )


def from_root(value, axis, source):
    kept = jnp.where(lax.axis_index(axis) == source, value, 0).astype(value.dtype)
    return lax.psum(kept, axis)


def cuts_of(width):
    tiles = width // LANES
    ends = [tiles * i // 4 * LANES for i in range(5)]
    return [(ends[i], ends[i + 1] - ends[i]) for i in range(4)]


def gather_kernel(count, own_ref, all_ref, send_sem, recv_sem, copy_sem):
    ring_size = count // 4
    half = ring_size // 2
    me = lax.axis_index("dp")
    ring, quad = me // 4, me % 4
    x_bit, y_bit = quad % 2, quad // 2
    quad_x = quad + 1 - 2 * x_bit
    quad_y = quad + 2 - 4 * y_bit
    quad_d = quad_x + 2 - 4 * y_bit
    cuts = cuts_of(own_ref.shape[1])

    def at(offset, q):
        return (ring + offset + ring_size) % ring_size * 4 + q

    up, down, across, along = at(1, quad), at(-1, quad), at(0, quad_x), at(0, quad_y)

    barrier = pltpu.get_barrier_semaphore()
    for peer in (up, down, across, along):
        pl.semaphore_signal(
            barrier, inc=1, device_id={"dp": peer}, device_id_type=pl.DeviceIdType.MESH
        )
    pl.semaphore_wait(barrier, 4)

    keep = pltpu.make_async_copy(own_ref, all_ref.at[me], copy_sem)
    keep.start()
    sent = []
    ports = {"up": (0, up), "down": (1, down), "across": (2, across), "along": (3, along)}

    def copy(piece, source, port, mine):
        lane, target = ports[port]
        start, size = cuts[piece]
        columns = pl.ds(start, size)
        from_ref = own_ref.at[:, columns] if mine else all_ref.at[source, :, columns]
        return pltpu.make_async_remote_copy(
            src_ref=from_ref,
            dst_ref=all_ref.at[source, :, columns],
            send_sem=send_sem.at[piece, source, lane],
            recv_sem=recv_sem.at[piece, source],
            device_id={"dp": target},
            device_id_type=pl.DeviceIdType.MESH,
        )

    def send(piece, source, port, mine=False):
        item = copy(piece, source, port, mine)
        item.start()
        sent.append(item)

    def arrive(piece, source):
        copy(piece, source, "up", False).wait_recv()

    def ring_step(piece, step, q, then=()):
        turn = piece % 2
        for sign, port, wins in ((-1, "up", 0), (1, "down", 1)):
            if step == half and turn != wins:
                continue
            source = at(sign * step, q)
            arrive(piece, source)
            if step + 1 < half or (step + 1 == half and turn == wins):
                send(piece, source, port)
            for other in then:
                send(piece, source, other)

    def square_step(piece, offset, first, then=()):
        turn = piece % 2
        if first:
            for q, port, wins in ((quad_x, "along", 0), (quad_y, "across", 1)):
                source = at(offset, q)
                arrive(piece, source)
                if turn == wins:
                    send(piece, source, port)
                for other in then:
                    send(piece, source, other)
        else:
            source = at(offset, quad_d)
            arrive(piece, source)
            for other in then:
                send(piece, source, other)

    both, flat = ("up", "down"), ("across", "along")
    for piece in (0, 1):
        for port in both:
            send(piece, me, port, True)
    for piece in (2, 3):
        for port in flat:
            send(piece, me, port, True)
    for piece in (2, 3):
        for port in both:
            send(piece, me, port, True)
    for piece in (0, 1):
        for port in flat:
            send(piece, me, port, True)
    for piece in (0, 1):
        ring_step(piece, 1, quad, flat)
    for piece in (2, 3):
        square_step(piece, 0, True, both)
    for piece in (2, 3):
        square_step(piece, 0, False, both)
    for piece in (0, 1):
        square_step(piece, 0, True)
    for step in range(2, half + 1):
        for piece in (0, 1):
            ring_step(piece, step, quad, flat)
    offsets = [sign * step for step in range(1, half) for sign in (-1, 1)] + [half]
    steps = range(1, half + 1)
    flat_work = [
        functools.partial(square_step, piece, offset, True)
        for offset in offsets
        for piece in (0, 1)
    ]
    ring_work = [
        functools.partial(ring_step, piece, step, q)
        for step in steps
        for q in (quad, quad_x, quad_y, quad_d)
        for piece in (2, 3)
    ]
    done = 0
    for index, work in enumerate(ring_work):
        work()
        goal = len(flat_work) * (index + 1) // len(ring_work)
        while done < goal:
            flat_work[done]()
            done += 1
    for offset in [0] + offsets:
        for piece in (0, 1):
            square_step(piece, offset, False)
    for item in sent:
        item.wait_send()
    keep.wait()


def gather(block):
    count = lax.axis_size("dp")
    rows, width = block.shape
    if count % 8 or count < 16:
        return lax.all_gather(block, "dp", axis=0, tiled=True)
    everything = pl.pallas_call(
        functools.partial(gather_kernel, count),
        out_shape=jax.ShapeDtypeStruct((count, rows, width), block.dtype),
        in_specs=[pl.BlockSpec(memory_space=pl.ANY)],
        out_specs=pl.BlockSpec(memory_space=pl.ANY),
        scratch_shapes=[
            pltpu.SemaphoreType.DMA((4, count, 4)),
            pltpu.SemaphoreType.DMA((4, count)),
            pltpu.SemaphoreType.DMA,
        ],
        compiler_params=pltpu.CompilerParams(collective_id=0, has_side_effects=True),
    )(block)
    return everything.reshape(count * rows, width)


def local(layer_input, up_weight, grad_output, factor_input, factor_grad, decay):
    ratio = lax.axis_size("dp") // lax.axis_size("tensor")
    own = lax.axis_index("dp")
    owner = own // ratio
    token_total = layer_input.shape[0] * lax.axis_size("dp")
    keep = decay[0]
    blend = (1.0 - keep) / token_total
    feat_rows = up_weight.shape[0]
    unit_rows = factor_grad.shape[0]
    units, feats = grad_output.shape[1], layer_input.shape[1]
    pad = -(units + feats) % LANES
    block = jnp.concatenate([grad_output, layer_input], axis=1)
    block = jnp.pad(block, ((0, 0), (0, pad)))
    everything = gather(block)
    grad_all = everything[:, :units]
    input_all = everything[:, units : units + feats]
    input_slice = lax.dynamic_slice_in_dim(input_all, own % ratio * feat_rows, feat_rows, 1)
    input_part = from_root(input_slice, "tensor", owner)
    gram_input = contract_rows(input_part, input_all)
    new_factor_input = keep * factor_input + blend * gram_input
    grad_slice = lax.dynamic_slice_in_dim(grad_all, own % ratio * unit_rows, unit_rows, 1)
    grad_part = from_root(grad_slice, "tensor", owner)
    grad_weight = contract_rows(input_part, grad_all)
    gram_grad = contract_rows(grad_part, grad_all)
    partial_in = contract_cols(grad_all, up_weight)
    new_factor_grad = keep * factor_grad + blend * gram_grad
    grad_input = lax.psum_scatter(partial_in, "tensor", scatter_dimension=0, tiled=True).astype(
        jnp.bfloat16
    )
    return (grad_weight, grad_input, new_factor_input, new_factor_grad)


def solution(mesh):
    return jax.shard_map(
        local,
        mesh=mesh,
        in_specs=(
            P("dp", "tensor"),
            P("dp", "tensor"),
            P("dp", "tensor"),
            P("dp", "tensor"),
            P("dp", "tensor"),
            P(),
        ),
        out_specs=(P("dp", "tensor"), P("tensor", "dp"), P("dp", "tensor"), P("dp", "tensor")),
        check_vma=False,
    )
```

```python
import functools

import jax
import jax.numpy as jnp
from jax import lax
from jax.experimental import pallas as pl
from jax.experimental.pallas import tpu as pltpu
from jax.sharding import PartitionSpec as P

LANES = 128


def contract_rows(left, right):
    return lax.dot_general(
        left, right, (((0,), (0,)), ((), ())), preferred_element_type=jnp.float32
    )


def contract_cols(left, right):
    return lax.dot_general(
        left, right, (((1,), (1,)), ((), ())), preferred_element_type=jnp.float32
    )


def pieces_of(start, tiles):
    long = tiles * 7 // 18
    short = tiles // 2 - long
    sizes = [long, tiles - long - 2 * short, short, short]
    edges = [start]
    for size in sizes:
        edges.append(edges[-1] + size)
    return [(edges[i] * LANES, sizes[i] * LANES) for i in range(4)]


def jobs_of(widths):
    jobs = []
    for array, width in enumerate(widths):
        tiles = width // LANES
        chunks = max(1, tiles // 18)
        for i in range(chunks):
            start, end = tiles * i // chunks, tiles * (i + 1) // chunks
            jobs.append((array, pieces_of(start, end - start)))
    return jobs


def window_of(own, size, width):
    wide = min(-(-(size + LANES) // LANES) * LANES, width)
    first = jnp.minimum(own * size // LANES * LANES, width - wide)
    return first, wide


def gather_kernel(count, cores, parts, *refs):
    own_refs, all_refs, win_refs = refs[:2], refs[2:4], refs[4:6]
    send_sem, recv_sem, copy_sem, win_send, win_recv = refs[6:]
    length = count // 4
    me = lax.axis_index("dp")
    core = lax.axis_index("tensor")
    line, quad = me // 4, me % 4
    x_bit, y_bit = quad % 2, quad // 2
    quad_x = quad + 1 - 2 * x_bit
    quad_y = quad + 2 - 4 * y_bit
    quad_d = quad_x + 2 - 4 * y_bit
    jobs = jobs_of([ref.shape[1] for ref in own_refs])

    def at(offset, q):
        return (line + offset + length) % length * 4 + q

    targets = [at(1, quad), at(-1, quad), at(0, quad_x), at(0, quad_y)]
    UP, DOWN, ACROSS, ALONG = range(4)
    has = {UP: line < length - 1, DOWN: line > 0}

    barrier = pltpu.get_barrier_semaphore()

    def greet(**where):
        pl.semaphore_signal(
            barrier, inc=1, device_id=where, device_id_type=pl.DeviceIdType.MESH
        )

    for target in targets:
        greet(dp=target)
    for hop in range(1, cores):
        greet(tensor=(core + hop) % cores)
    pl.semaphore_wait(barrier, 4 + cores - 1)

    keeps = [
        pltpu.make_async_copy(own, everything.at[me], copy_sem.at[i])
        for i, (own, everything) in enumerate(zip(own_refs, all_refs))
    ]
    for keep in keeps:
        keep.start()
    sent = []

    def copy(job, piece, source, port, mine=False):
        array, pieces = jobs[job]
        start, size = pieces[piece]
        columns = pl.ds(start, size)
        from_ref = own_refs[array].at[:, columns] if mine else all_refs[array].at[source, :, columns]
        return pltpu.make_async_remote_copy(
            src_ref=from_ref,
            dst_ref=all_refs[array].at[source, :, columns],
            send_sem=send_sem.at[job, piece, source, port],
            recv_sem=recv_sem.at[job, piece, source],
            device_id={"dp": targets[port]},
            device_id_type=pl.DeviceIdType.MESH,
        )

    def under(condition, work):
        if condition is None:
            work()
        else:
            pl.when(condition)(work)

    def both_of(first, second):
        if first is None or second is None:
            return second if first is None else first
        return jnp.logical_and(first, second)

    def send(job, piece, source, ports, exists=None, mine=False):
        for port in ports:
            item = copy(job, piece, source, port, mine)
            condition = both_of(exists, has.get(port))
            under(condition, item.start)
            sent.append((condition, item))

    def arrive(job, piece, source, exists=None):
        under(exists, lambda: copy(job, piece, source, UP).wait_recv())

    def seen(offset):
        if offset == 0:
            return None
        return line >= -offset if offset < 0 else line < length - offset

    def line_step(job, piece, offset, q, then=()):
        source, exists = at(offset, q), seen(offset)
        arrive(job, piece, source, exists)
        send(job, piece, source, (UP if offset < 0 else DOWN,) + tuple(then), exists)

    def square_step(job, piece, offset, q, port, then=()):
        source, exists = at(offset, q), seen(offset)
        arrive(job, piece, source, exists)
        send(job, piece, source, (() if port is None else (port,)) + tuple(then), exists)

    zed, flat = (UP, DOWN), (ACROSS, ALONG)
    offsets = [sign * step for step in range(1, length) for sign in (-1, 1)]

    def start_of(job):
        for pieces, ports in (((0, 1), zed), ((2, 3), flat), ((2, 3), zed), ((0, 1), flat)):
            for piece in pieces:
                send(job, piece, me, ports, mine=True)

    def steps_of(job):
        def near(piece, offset, then=()):
            turn = piece % 2
            square_step(job, piece, offset, quad_x, ALONG if turn == 0 else None, then)
            square_step(job, piece, offset, quad_y, ACROSS if turn == 1 else None, then)

        steps = []

        def add(work, *args):
            steps.append(functools.partial(work, *args))

        for piece in (2, 3):
            add(near, piece, 0, zed)
        for offset in offsets[:2]:
            for piece in (0, 1):
                add(line_step, job, piece, offset, quad, flat)
        for piece in (2, 3):
            add(square_step, job, piece, 0, quad_d, None, zed)
        for piece in (0, 1):
            add(near, piece, 0)
        for offset in offsets[:2]:
            for q in (quad, quad_x):
                for piece in (2, 3):
                    add(line_step, job, piece, offset, q)
            for piece in (0, 1):
                add(near, piece, offset)
        for piece in (0, 1):
            add(square_step, job, piece, 0, quad_d, None)
        for index in range(2, len(offsets) + 2, 2):
            later = offsets[index : index + 2]
            for offset in later:
                for piece in (0, 1):
                    add(line_step, job, piece, offset, quad, flat)
            for offset in offsets[index - 2 : index]:
                for q in (quad_y, quad_d):
                    for piece in (2, 3):
                        add(line_step, job, piece, offset, q)
                for piece in (0, 1):
                    add(square_step, job, piece, offset, quad_d, None)
            for offset in later:
                for q in (quad, quad_x):
                    for piece in (2, 3):
                        add(line_step, job, piece, offset, q)
                for piece in (0, 1):
                    add(near, piece, offset)
        return steps

    ratio = count // cores
    owner = me // ratio
    windows = []
    for array in range(2):
        first, wide = window_of(me % ratio, parts[array], all_refs[array].shape[2])
        first = pl.multiple_of(first, LANES)
        hops = []
        for hop in range(1, cores):
            hops.append(
                pltpu.make_async_remote_copy(
                    src_ref=all_refs[array].at[:, :, pl.ds(first, wide)],
                    dst_ref=win_refs[array],
                    send_sem=win_send.at[array, hop],
                    recv_sem=win_recv.at[array],
                    device_id={"tensor": (core + hop) % cores},
                    device_id_type=pl.DeviceIdType.MESH,
                )
            )
        windows.append(hops)

    def share(array):
        keeps[array].wait()

        @pl.when(core == owner)
        def _():
            for hop in windows[array]:
                hop.start()

    for job in range(len(jobs)):
        start_of(job)
    plan = []
    for job in range(len(jobs)):
        steps = steps_of(job)
        for index, work in enumerate(steps):
            plan.append((index + job * 0.6 * len(steps), job, index == len(steps) - 1, work))
    plan.sort(key=lambda entry: entry[:2])
    left = [sum(1 for array, _ in jobs if array == i) for i in range(2)]
    for _, job, last, work in plan:
        work()
        if last:
            array = jobs[job][0]
            left[array] -= 1
            if left[array] == 0:
                share(array)
    for condition, item in sent:
        under(condition, item.wait_send)
    for hops in windows:

        @pl.when(core == owner)
        def _():
            for hop in hops:
                hop.wait_send()

        @pl.when(core != owner)
        def _():
            hops[0].wait_recv()


def gather(blocks, parts):
    count, cores = lax.axis_size("dp"), lax.axis_size("tensor")
    rows = blocks[0].shape[0]
    widths = [block.shape[1] for block in blocks]
    blocks = [jnp.pad(block, ((0, 0), (0, -block.shape[1] % LANES))) for block in blocks]
    own = lax.axis_index("dp") % (count // cores)
    spans = [window_of(own, part, block.shape[1]) for part, block in zip(parts, blocks)]
    jobs = len(jobs_of([block.shape[1] for block in blocks]))
    shapes = [block.shape[1] for block in blocks] + [wide for _, wide in spans]
    results = pl.pallas_call(
        functools.partial(gather_kernel, count, cores, parts),
        out_shape=[
            jax.ShapeDtypeStruct((count, rows, width), blocks[0].dtype) for width in shapes
        ],
        in_specs=[pl.BlockSpec(memory_space=pl.ANY)] * 2,
        out_specs=[pl.BlockSpec(memory_space=pl.ANY)] * 4,
        scratch_shapes=[
            pltpu.SemaphoreType.DMA((jobs, 4, count, 4)),
            pltpu.SemaphoreType.DMA((jobs, 4, count)),
            pltpu.SemaphoreType.DMA((2,)),
            pltpu.SemaphoreType.DMA((2, cores)),
            pltpu.SemaphoreType.DMA((2,)),
        ],
        compiler_params=pltpu.CompilerParams(collective_id=0, has_side_effects=True),
    )(*blocks)
    flat = [result.reshape(count * rows, result.shape[2]) for result in results]
    here = lax.axis_index("tensor") == lax.axis_index("dp") // (count // cores)
    slices = []
    for everything, window, part, (first, wide) in zip(flat[:2], flat[2:], parts, spans):
        mine = lax.dynamic_slice_in_dim(everything, own * part, part, 1)
        other = lax.dynamic_slice_in_dim(window, own * part - first, part, 1)
        slices.append(jnp.where(here, mine, other))
    whole = [everything[:, :width] for everything, width in zip(flat[:2], widths)]
    return whole, slices


def local(layer_input, up_weight, grad_output, factor_input, factor_grad, decay):
    token_total = layer_input.shape[0] * lax.axis_size("dp")
    keep = decay[0]
    blend = (1.0 - keep) / token_total
    feat_rows = up_weight.shape[0]
    unit_rows = factor_grad.shape[0]
    (input_all, grad_all), (input_part, grad_part) = gather(
        (layer_input, grad_output), (feat_rows, unit_rows)
    )
    gram_input = contract_rows(input_part, input_all)
    new_factor_input = keep * factor_input + blend * gram_input
    grad_weight = contract_rows(input_part, grad_all)
    gram_grad = contract_rows(grad_part, grad_all)
    partial_in = contract_cols(grad_all, up_weight)
    new_factor_grad = keep * factor_grad + blend * gram_grad
    grad_input = lax.psum_scatter(partial_in, "tensor", scatter_dimension=0, tiled=True).astype(
        jnp.bfloat16
    )
    return (grad_weight, grad_input, new_factor_input, new_factor_grad)


def solution(mesh):
    return jax.shard_map(
        local,
        mesh=mesh,
        in_specs=(
            P("dp", "tensor"),
            P("dp", "tensor"),
            P("dp", "tensor"),
            P("dp", "tensor"),
            P("dp", "tensor"),
            P(),
        ),
        out_specs=(P("dp", "tensor"), P("tensor", "dp"), P("dp", "tensor"), P("dp", "tensor")),
        check_vma=False,
    )
```

```python
import functools

import jax
import jax.numpy as jnp
from jax import lax
from jax.experimental import pallas as pl
from jax.experimental.pallas import tpu as pltpu
from jax.sharding import PartitionSpec as P

LANES = 128


def contract_rows(left, right):
    return lax.dot_general(
        left, right, (((0,), (0,)), ((), ())), preferred_element_type=jnp.float32
    )


def contract_cols(left, right):
    return lax.dot_general(
        left, right, (((1,), (1,)), ((), ())), preferred_element_type=jnp.float32
    )


def pieces_of(start, tiles):
    long = tiles * 7 // 18
    short = tiles // 2 - long
    sizes = [long, tiles - long - 2 * short, short, short]
    edges = [start]
    for size in sizes:
        edges.append(edges[-1] + size)
    return [(edges[i] * LANES, sizes[i] * LANES) for i in range(4)]


def jobs_of(widths):
    jobs = []
    for array, width in enumerate(widths):
        tiles = width // LANES
        chunks = max(1, tiles // 18)
        for i in range(chunks):
            start, end = tiles * i // chunks, tiles * (i + 1) // chunks
            jobs.append((array, pieces_of(start, end - start)))
    return jobs


def window_of(own, size, width):
    wide = min(-(-(size + LANES) // LANES) * LANES, width)
    first = jnp.minimum(own * size // LANES * LANES, width - wide)
    return first, wide


def gather_kernel(count, cores, parts, *refs):
    own_refs, all_refs, win_refs = refs[:2], refs[2:4], refs[4:6]
    send_sem, recv_sem, copy_sem, win_send, win_recv = refs[6:]
    length = count // 4
    me = lax.axis_index("dp")
    core = lax.axis_index("tensor")
    line, quad = me // 4, me % 4
    x_bit, y_bit = quad % 2, quad // 2
    quad_x = quad + 1 - 2 * x_bit
    quad_y = quad + 2 - 4 * y_bit
    quad_d = quad_x + 2 - 4 * y_bit
    jobs = jobs_of([ref.shape[1] for ref in own_refs])

    def at(offset, q):
        return (line + offset + length) % length * 4 + q

    targets = [at(1, quad), at(-1, quad), at(0, quad_x), at(0, quad_y)]
    UP, DOWN, ACROSS, ALONG = range(4)
    has = {UP: line < length - 1, DOWN: line > 0}

    barrier = pltpu.get_barrier_semaphore()

    def greet(**where):
        pl.semaphore_signal(
            barrier, inc=1, device_id=where, device_id_type=pl.DeviceIdType.MESH
        )

    for target in targets:
        greet(dp=target)
    for hop in range(1, cores):
        greet(tensor=(core + hop) % cores)
    pl.semaphore_wait(barrier, 4 + cores - 1)

    keeps = [
        pltpu.make_async_copy(own, everything.at[me], copy_sem.at[i])
        for i, (own, everything) in enumerate(zip(own_refs, all_refs))
    ]
    for keep in keeps:
        keep.start()
    sent = []

    def copy(job, piece, source, port, mine=False):
        array, pieces = jobs[job]
        start, size = pieces[piece]
        columns = pl.ds(start, size)
        from_ref = own_refs[array].at[:, columns] if mine else all_refs[array].at[source, :, columns]
        return pltpu.make_async_remote_copy(
            src_ref=from_ref,
            dst_ref=all_refs[array].at[source, :, columns],
            send_sem=send_sem.at[job, piece, source, port],
            recv_sem=recv_sem.at[job, piece, source],
            device_id={"dp": targets[port]},
            device_id_type=pl.DeviceIdType.MESH,
        )

    def under(condition, work):
        if condition is None:
            work()
        else:
            pl.when(condition)(work)

    def both_of(first, second):
        if first is None or second is None:
            return second if first is None else first
        return jnp.logical_and(first, second)

    def send(job, piece, source, ports, exists=None, mine=False):
        for port in ports:
            item = copy(job, piece, source, port, mine)
            condition = both_of(exists, has.get(port))
            under(condition, item.start)
            sent.append((condition, item))

    def arrive(job, piece, source, exists=None):
        under(exists, lambda: copy(job, piece, source, UP).wait_recv())

    def seen(offset):
        if offset == 0:
            return None
        return line >= -offset if offset < 0 else line < length - offset

    def line_step(job, piece, offset, q, then=()):
        source, exists = at(offset, q), seen(offset)
        arrive(job, piece, source, exists)
        send(job, piece, source, (UP if offset < 0 else DOWN,) + tuple(then), exists)

    def square_step(job, piece, offset, q, port, then=()):
        source, exists = at(offset, q), seen(offset)
        arrive(job, piece, source, exists)
        send(job, piece, source, (() if port is None else (port,)) + tuple(then), exists)

    zed, flat = (UP, DOWN), (ACROSS, ALONG)
    offsets = [sign * step for step in range(1, length) for sign in (-1, 1)]

    def start_of(job):
        for pieces, ports in (((0, 1), zed), ((2, 3), flat), ((2, 3), zed), ((0, 1), flat)):
            for piece in pieces:
                send(job, piece, me, ports, mine=True)

    def steps_of(job):
        def near(piece, offset, then=()):
            turn = piece % 2
            square_step(job, piece, offset, quad_x, ALONG if turn == 0 else None, then)
            square_step(job, piece, offset, quad_y, ACROSS if turn == 1 else None, then)

        steps = []

        def add(work, *args):
            offset = args[1] if work is near else args[2]
            steps.append((offset, functools.partial(work, *args)))

        for piece in (2, 3):
            add(near, piece, 0, zed)
        for offset in offsets[:2]:
            for piece in (0, 1):
                add(line_step, job, piece, offset, quad, flat)
        for piece in (2, 3):
            add(square_step, job, piece, 0, quad_d, None, zed)
        for piece in (0, 1):
            add(near, piece, 0)
        for offset in offsets[:2]:
            for q in (quad, quad_x):
                for piece in (2, 3):
                    add(line_step, job, piece, offset, q)
            for piece in (0, 1):
                add(near, piece, offset)
        for piece in (0, 1):
            add(square_step, job, piece, 0, quad_d, None)
        for index in range(2, len(offsets) + 2, 2):
            later = offsets[index : index + 2]
            for offset in later:
                for piece in (0, 1):
                    add(line_step, job, piece, offset, quad, flat)
            for offset in offsets[index - 2 : index]:
                for q in (quad_y, quad_d):
                    for piece in (2, 3):
                        add(line_step, job, piece, offset, q)
                for piece in (0, 1):
                    add(square_step, job, piece, offset, quad_d, None)
            for offset in later:
                for q in (quad, quad_x):
                    for piece in (2, 3):
                        add(line_step, job, piece, offset, q)
                for piece in (0, 1):
                    add(near, piece, offset)
        return steps

    ratio = count // cores
    owner = me // ratio
    windows = []

    def share(array, offset):
        if offset == 0:
            keeps[array].wait()
        first, wide = window_of(me % ratio, parts[array], all_refs[array].shape[2])
        columns = pl.ds(pl.multiple_of(first, LANES), wide)
        place = (line + offset + length) % length
        rows = pl.ds(place * 4, 4)
        for hop in range(1, cores):
            item = pltpu.make_async_remote_copy(
                src_ref=all_refs[array].at[rows, :, columns],
                dst_ref=win_refs[array].at[rows],
                send_sem=win_send.at[array, hop, place],
                recv_sem=win_recv.at[array, place],
                device_id={"tensor": (core + hop) % cores},
                device_id_type=pl.DeviceIdType.MESH,
            )
            under(both_of(seen(offset), core == owner), item.start)
            windows.append((offset, hop, item))

    for job in range(len(jobs)):
        start_of(job)
    plan = []
    for job in range(len(jobs)):
        steps = steps_of(job)
        for index, (offset, work) in enumerate(steps):
            plan.append((index + job * 0.6 * len(steps), job, offset, work))
    plan.sort(key=lambda entry: entry[:2])
    left = {}
    for _, job, offset, _ in plan:
        key = jobs[job][0], offset
        left[key] = left.get(key, 0) + 1
    for _, job, offset, work in plan:
        work()
        key = jobs[job][0], offset
        left[key] -= 1
        if left[key] == 0:
            share(*key)
    for condition, item in sent:
        under(condition, item.wait_send)
    for offset, hop, item in windows:
        under(both_of(seen(offset), core == owner), item.wait_send)
        if hop == 1:
            under(both_of(seen(offset), core != owner), item.wait_recv)


def gather(blocks, parts):
    count, cores = lax.axis_size("dp"), lax.axis_size("tensor")
    rows = blocks[0].shape[0]
    widths = [block.shape[1] for block in blocks]
    blocks = [jnp.pad(block, ((0, 0), (0, -block.shape[1] % LANES))) for block in blocks]
    own = lax.axis_index("dp") % (count // cores)
    spans = [window_of(own, part, block.shape[1]) for part, block in zip(parts, blocks)]
    jobs = len(jobs_of([block.shape[1] for block in blocks]))
    shapes = [block.shape[1] for block in blocks] + [wide for _, wide in spans]
    results = pl.pallas_call(
        functools.partial(gather_kernel, count, cores, parts),
        out_shape=[
            jax.ShapeDtypeStruct((count, rows, width), blocks[0].dtype) for width in shapes
        ],
        in_specs=[pl.BlockSpec(memory_space=pl.ANY)] * 2,
        out_specs=[pl.BlockSpec(memory_space=pl.ANY)] * 4,
        scratch_shapes=[
            pltpu.SemaphoreType.DMA((jobs, 4, count, 4)),
            pltpu.SemaphoreType.DMA((jobs, 4, count)),
            pltpu.SemaphoreType.DMA((2,)),
            pltpu.SemaphoreType.DMA((2, cores, count // 4)),
            pltpu.SemaphoreType.DMA((2, count // 4)),
        ],
        compiler_params=pltpu.CompilerParams(collective_id=0, has_side_effects=True),
    )(*blocks)
    flat = [result.reshape(count * rows, result.shape[2]) for result in results]
    here = lax.axis_index("tensor") == lax.axis_index("dp") // (count // cores)
    slices = []
    for everything, window, part, (first, wide) in zip(flat[:2], flat[2:], parts, spans):
        mine = lax.dynamic_slice_in_dim(everything, own * part, part, 1)
        other = lax.dynamic_slice_in_dim(window, own * part - first, part, 1)
        slices.append(jnp.where(here, mine, other))
    whole = [everything[:, :width] for everything, width in zip(flat[:2], widths)]
    return whole, slices


def scatter_sum(value, axis):
    size, me = lax.axis_size(axis), lax.axis_index(axis)
    rows = value.shape[0] // size
    total = lax.dynamic_slice_in_dim(value, me * rows, rows, 0)
    for hop in range(1, size):
        share = lax.dynamic_slice_in_dim(value, (me + hop) % size * rows, rows, 0)
        ring = [(i, (i + hop) % size) for i in range(size)]
        total = total + lax.ppermute(share, axis, ring)
    return total


def local(layer_input, up_weight, grad_output, factor_input, factor_grad, decay):
    token_total = layer_input.shape[0] * lax.axis_size("dp")
    keep = decay[0]
    blend = (1.0 - keep) / token_total
    feat_rows = up_weight.shape[0]
    unit_rows = factor_grad.shape[0]
    (input_all, grad_all), (input_part, grad_part) = gather(
        (layer_input, grad_output), (feat_rows, unit_rows)
    )
    gram_input = contract_rows(input_part, input_all)
    new_factor_input = keep * factor_input + blend * gram_input
    grad_weight = contract_rows(input_part, grad_all)
    gram_grad = contract_rows(grad_part, grad_all)
    partial_in = contract_cols(grad_all, up_weight)
    new_factor_grad = keep * factor_grad + blend * gram_grad
    grad_input = scatter_sum(partial_in, "tensor").astype(jnp.bfloat16)
    return (grad_weight, grad_input, new_factor_input, new_factor_grad)


def solution(mesh):
    return jax.shard_map(
        local,
        mesh=mesh,
        in_specs=(
            P("dp", "tensor"),
            P("dp", "tensor"),
            P("dp", "tensor"),
            P("dp", "tensor"),
            P("dp", "tensor"),
            P(),
        ),
        out_specs=(P("dp", "tensor"), P("tensor", "dp"), P("dp", "tensor"), P("dp", "tensor")),
        check_vma=False,
    )
```

```python
import functools

import jax
import jax.numpy as jnp
from jax import lax
from jax.experimental import pallas as pl
from jax.experimental.pallas import tpu as pltpu
from jax.sharding import PartitionSpec as P

LANES = 128


def contract_rows(left, right):
    return lax.dot_general(
        left, right, (((0,), (0,)), ((), ())), preferred_element_type=jnp.float32
    )


def contract_cols(left, right):
    return lax.dot_general(
        left, right, (((1,), (1,)), ((), ())), preferred_element_type=jnp.float32
    )


def pieces_of(start, tiles):
    long = tiles * 7 // 18
    short = tiles // 2 - long
    sizes = [long, tiles - long - 2 * short, short, short]
    edges = [start]
    for size in sizes:
        edges.append(edges[-1] + size)
    return [(edges[i] * LANES, sizes[i] * LANES) for i in range(4)]


def jobs_of(widths):
    jobs = []
    for array, width in enumerate(widths):
        tiles = width // LANES
        chunks = max(1, tiles // 108)
        for i in range(chunks):
            start, end = tiles * i // chunks, tiles * (i + 1) // chunks
            jobs.append((array, pieces_of(start, end - start)))
    return jobs


def window_of(own, size, width):
    wide = min(-(-(size + LANES) // LANES) * LANES, width)
    first = jnp.minimum(own * size // LANES * LANES, width - wide)
    return first, wide


def gather_kernel(count, cores, parts, *refs):
    own_refs, all_refs, win_refs = refs[:2], refs[2:4], refs[4:6]
    send_sem, recv_sem, copy_sem, win_send, win_recv = refs[6:]
    length = count // 4
    me = lax.axis_index("dp")
    core = lax.axis_index("tensor")
    line, quad = me // 4, me % 4
    x_bit, y_bit = quad % 2, quad // 2
    quad_x = quad + 1 - 2 * x_bit
    quad_y = quad + 2 - 4 * y_bit
    quad_d = quad_x + 2 - 4 * y_bit
    jobs = jobs_of([ref.shape[1] for ref in own_refs])

    def at(offset, q):
        return (line + offset + length) % length * 4 + q

    targets = [at(1, quad), at(-1, quad), at(0, quad_x), at(0, quad_y)]
    UP, DOWN, ACROSS, ALONG = range(4)
    has = {UP: line < length - 1, DOWN: line > 0}

    barrier = pltpu.get_barrier_semaphore()

    def greet(**where):
        pl.semaphore_signal(
            barrier, inc=1, device_id=where, device_id_type=pl.DeviceIdType.MESH
        )

    for target in targets:
        greet(dp=target)
    for hop in range(1, cores):
        greet(tensor=(core + hop) % cores)
    pl.semaphore_wait(barrier, 4 + cores - 1)

    keeps = [
        pltpu.make_async_copy(own, everything.at[me], copy_sem.at[i])
        for i, (own, everything) in enumerate(zip(own_refs, all_refs))
    ]
    for keep in keeps:
        keep.start()
    sent = []

    def copy(job, piece, source, port, mine=False):
        array, pieces = jobs[job]
        start, size = pieces[piece]
        columns = pl.ds(start, size)
        from_ref = own_refs[array].at[:, columns] if mine else all_refs[array].at[source, :, columns]
        return pltpu.make_async_remote_copy(
            src_ref=from_ref,
            dst_ref=all_refs[array].at[source, :, columns],
            send_sem=send_sem.at[job, piece, source, port],
            recv_sem=recv_sem.at[job, piece, source],
            device_id={"dp": targets[port]},
            device_id_type=pl.DeviceIdType.MESH,
        )

    def under(condition, work):
        if condition is None:
            work()
        else:
            pl.when(condition)(work)

    def both_of(first, second):
        if first is None or second is None:
            return second if first is None else first
        return jnp.logical_and(first, second)

    def send(job, piece, source, ports, exists=None, mine=False):
        for port in ports:
            item = copy(job, piece, source, port, mine)
            condition = both_of(exists, has.get(port))
            under(condition, item.start)
            sent.append((condition, item))

    def arrive(job, piece, source, exists=None):
        under(exists, lambda: copy(job, piece, source, UP).wait_recv())

    def seen(offset):
        if offset == 0:
            return None
        return line >= -offset if offset < 0 else line < length - offset

    def line_step(job, piece, offset, q, then=()):
        source, exists = at(offset, q), seen(offset)
        arrive(job, piece, source, exists)
        send(job, piece, source, (UP if offset < 0 else DOWN,) + tuple(then), exists)

    def square_step(job, piece, offset, q, port, then=()):
        source, exists = at(offset, q), seen(offset)
        arrive(job, piece, source, exists)
        send(job, piece, source, (() if port is None else (port,)) + tuple(then), exists)

    zed, flat = (UP, DOWN), (ACROSS, ALONG)
    offsets = [sign * step for step in range(1, length) for sign in (-1, 1)]

    def start_of(job):
        for pieces, ports in (((0, 1), zed), ((2, 3), flat), ((2, 3), zed), ((0, 1), flat)):
            for piece in pieces:
                send(job, piece, me, ports, mine=True)

    def steps_of(job):
        def near(piece, offset, then=()):
            turn = piece % 2
            square_step(job, piece, offset, quad_x, ALONG if turn == 0 else None, then)
            square_step(job, piece, offset, quad_y, ACROSS if turn == 1 else None, then)

        steps = []

        def add(work, *args):
            offset = args[1] if work is near else args[2]
            steps.append((offset, functools.partial(work, *args)))

        for piece in (2, 3):
            add(near, piece, 0, zed)
        for offset in offsets[:2]:
            for piece in (0, 1):
                add(line_step, job, piece, offset, quad, flat)
        for piece in (2, 3):
            add(square_step, job, piece, 0, quad_d, None, zed)
        for piece in (0, 1):
            add(near, piece, 0)
        for offset in offsets[:2]:
            for q in (quad, quad_x):
                for piece in (2, 3):
                    add(line_step, job, piece, offset, q)
            for piece in (0, 1):
                add(near, piece, offset)
        for piece in (0, 1):
            add(square_step, job, piece, 0, quad_d, None)
        for index in range(2, len(offsets) + 2, 2):
            later = offsets[index : index + 2]
            for offset in later:
                for piece in (0, 1):
                    add(line_step, job, piece, offset, quad, flat)
            for offset in offsets[index - 2 : index]:
                for q in (quad_y, quad_d):
                    for piece in (2, 3):
                        add(line_step, job, piece, offset, q)
                for piece in (0, 1):
                    add(square_step, job, piece, offset, quad_d, None)
            for offset in later:
                for q in (quad, quad_x):
                    for piece in (2, 3):
                        add(line_step, job, piece, offset, q)
                for piece in (0, 1):
                    add(near, piece, offset)
        return steps

    ratio = count // cores
    owner = me // ratio
    windows = []

    def share(array, offset):
        if offset == 0:
            keeps[array].wait()
        first, wide = window_of(me % ratio, parts[array], all_refs[array].shape[2])
        columns = pl.ds(pl.multiple_of(first, LANES), wide)
        place = (line + offset + length) % length
        rows = pl.ds(place * 4, 4)
        for hop in range(1, cores):
            item = pltpu.make_async_remote_copy(
                src_ref=all_refs[array].at[rows, :, columns],
                dst_ref=win_refs[array].at[rows],
                send_sem=win_send.at[array, hop, place],
                recv_sem=win_recv.at[array, place],
                device_id={"tensor": (core + hop) % cores},
                device_id_type=pl.DeviceIdType.MESH,
            )
            under(both_of(seen(offset), core == owner), item.start)
            windows.append((offset, hop, item))

    for job in range(len(jobs)):
        start_of(job)
    plan = []
    for job in range(len(jobs)):
        steps = steps_of(job)
        for index, (offset, work) in enumerate(steps):
            plan.append((index + job * 0.6 * len(steps), job, offset, work))
    plan.sort(key=lambda entry: entry[:2])
    left = {}
    for _, job, offset, _ in plan:
        key = jobs[job][0], offset
        left[key] = left.get(key, 0) + 1
    for _, job, offset, work in plan:
        work()
        key = jobs[job][0], offset
        left[key] -= 1
        if left[key] == 0:
            share(*key)
    for condition, item in sent:
        under(condition, item.wait_send)
    for offset, hop, item in windows:
        under(both_of(seen(offset), core == owner), item.wait_send)
        if hop == 1:
            under(both_of(seen(offset), core != owner), item.wait_recv)


def gather(blocks, parts):
    count, cores = lax.axis_size("dp"), lax.axis_size("tensor")
    rows = blocks[0].shape[0]
    widths = [block.shape[1] for block in blocks]
    blocks = [jnp.pad(block, ((0, 0), (0, -block.shape[1] % LANES))) for block in blocks]
    own = lax.axis_index("dp") % (count // cores)
    spans = [window_of(own, part, block.shape[1]) for part, block in zip(parts, blocks)]
    jobs = len(jobs_of([block.shape[1] for block in blocks]))
    shapes = [block.shape[1] for block in blocks] + [wide for _, wide in spans]
    results = pl.pallas_call(
        functools.partial(gather_kernel, count, cores, parts),
        out_shape=[
            jax.ShapeDtypeStruct((count, rows, width), blocks[0].dtype) for width in shapes
        ],
        in_specs=[pl.BlockSpec(memory_space=pl.ANY)] * 2,
        out_specs=[pl.BlockSpec(memory_space=pl.ANY)] * 4,
        scratch_shapes=[
            pltpu.SemaphoreType.DMA((jobs, 4, count, 4)),
            pltpu.SemaphoreType.DMA((jobs, 4, count)),
            pltpu.SemaphoreType.DMA((2,)),
            pltpu.SemaphoreType.DMA((2, cores, count // 4)),
            pltpu.SemaphoreType.DMA((2, count // 4)),
        ],
        compiler_params=pltpu.CompilerParams(collective_id=0, has_side_effects=True),
    )(*blocks)
    flat = [result.reshape(count * rows, result.shape[2]) for result in results]
    here = lax.axis_index("tensor") == lax.axis_index("dp") // (count // cores)
    slices = []
    for everything, window, part, (first, wide) in zip(flat[:2], flat[2:], parts, spans):
        mine = lax.dynamic_slice_in_dim(everything, own * part, part, 1)
        other = lax.dynamic_slice_in_dim(window, own * part - first, part, 1)
        slices.append(jnp.where(here, mine, other))
    whole = [everything[:, :width] for everything, width in zip(flat[:2], widths)]
    return whole, slices


def scatter_sum(value, axis):
    size, me = lax.axis_size(axis), lax.axis_index(axis)
    rows = value.shape[0] // size
    total = lax.dynamic_slice_in_dim(value, me * rows, rows, 0)
    for hop in range(1, size):
        share = lax.dynamic_slice_in_dim(value, (me + hop) % size * rows, rows, 0)
        ring = [(i, (i + hop) % size) for i in range(size)]
        total = total + lax.ppermute(share, axis, ring)
    return total


def local(layer_input, up_weight, grad_output, factor_input, factor_grad, decay):
    token_total = layer_input.shape[0] * lax.axis_size("dp")
    keep = decay[0]
    blend = (1.0 - keep) / token_total
    feat_rows = up_weight.shape[0]
    unit_rows = factor_grad.shape[0]
    (input_all, grad_all), (input_part, grad_part) = gather(
        (layer_input, grad_output), (feat_rows, unit_rows)
    )
    gram_input = contract_rows(input_part, input_all)
    new_factor_input = keep * factor_input + blend * gram_input
    grad_weight = contract_rows(input_part, grad_all)
    gram_grad = contract_rows(grad_part, grad_all)
    partial_in = contract_cols(grad_all, up_weight)
    new_factor_grad = keep * factor_grad + blend * gram_grad
    grad_input = scatter_sum(partial_in, "tensor").astype(jnp.bfloat16)
    return (grad_weight, grad_input, new_factor_input, new_factor_grad)


def solution(mesh):
    return jax.shard_map(
        local,
        mesh=mesh,
        in_specs=(
            P("dp", "tensor"),
            P("dp", "tensor"),
            P("dp", "tensor"),
            P("dp", "tensor"),
            P("dp", "tensor"),
            P(),
        ),
        out_specs=(P("dp", "tensor"), P("tensor", "dp"), P("dp", "tensor"), P("dp", "tensor")),
        check_vma=False,
    )
```
